512 devices in a mesh: site: 16 (over z), fault: 32 (over x, y, core).
Axes of the slice: x: 4, y: 4, z: 16, core: 2. Of those that a mesh axis runs over, the one named last changes fastest.
Arguments:
- green_tensor: bfloat16 [16, 512, 96, 6, 256], P('site', 'fault'), may hold values from -0.375 to 0.375
- slip_map: bfloat16 [512, 8, 256], P('fault', None, 'site'), may hold values from 0.19921875 to 2
- rupture_time: float32 [512, 8, 256], P('fault', None, 'site'), may hold values from 0 to 48
- variation_ids: int32 [512, 8], P('fault'), may hold values from 0 to 7, each once within a row
- variation_count: int32 [512], P('fault'), may hold values from 2 to 8, as said below
- tile_rupture: int32 [512], P('fault'), may hold values from 0 to 31
- owner_slot: int32 [32], replicated, may hold values from 0 to 31, each once
Outputs:
- seismograms: float32 [32, 8, 16, 3, 192], P('fault', None, 'site')
The draws below stay inside these ranges and needn't reach their ends.
Inputs may be any that keep to these rules, and one draw needn't show every extreme that they name: `variation_count`: every tile lists at least 2 of the 8 variations, and in every draw some tile lists all 8.
All inputs are finite; a program needn't handle non-finite values.
Results may differ from the reference program's by a relative error of at most 0.0027.
Values sent between devices are 32-bit elements; how exact they have to be, the bound alone decides.
No kernel may reach another device: no remote copies, remote signals or barrier semaphores. Data moves between devices by JAX's collectives and lax.ppermute only.
A program may use at most 64 MiB of HBM per device.

```python
import math
import jax
import jax.numpy as jnp
from jax import lax

P_SIZE = 256
F = 96
C = 3
VMAX = 8
NT = 192
SITES = 16
TILES = 512
RUPT = 32


def draw_variation_count(key, part):
    first_key, second_key = jax.random.split(jax.random.fold_in(key, 7))
    counts = jax.random.randint(first_key, (TILES,), VMAX // 3, VMAX + 1)
    full_tile = jax.random.randint(second_key, (), 0, TILES)
    return counts.at[full_tile].set(VMAX).astype(jnp.int32)


def place_ends(entries, rng, smallest, top_value):
    longest = entries.shape.index(max(entries.shape))
    spots = []
    for shift in (0, 1):
        where = [jax.random.randint(jax.random.fold_in(rng, axis), (), 0, length) for axis, length in enumerate(entries.shape)]
        where[longest] = (where[longest] + shift) % entries.shape[longest]
        spots.append(tuple(where))
    return entries.at[spots[0]].set(smallest).at[spots[1]].set(top_value)


def block_levels(stream_key, shape, cuts, smallest, high):
    level, own = 1.0, jax.random.fold_in(stream_key, 6)
    for axis_at, blocks in cuts:
        draws = jnp.exp(jax.random.uniform(jax.random.fold_in(own, axis_at), (blocks,), jnp.float32, smallest / len(cuts), high / len(cuts)))
        level = level * jnp.repeat(draws, shape[axis_at] // blocks).reshape([-1 if axis == axis_at else 1 for axis in range(len(shape))])
    return level


def scatter_about(own_key, dims, spread, most, cuts=(), kind=jnp.bfloat16):
    factor_of = block_levels(own_key, dims, cuts, -0.22, 0.18) if cuts else 1.0
    result = jax.random.normal(own_key, dims, jnp.float32) * spread * factor_of
    return jnp.minimum(jnp.maximum(result, -most), most).astype(kind)


def setup_inputs(seed: int = 0) -> dict:
    arg_keys = jax.random.split(jax.random.key(seed), 8)
    green_tensor = scatter_about(arg_keys[0], (SITES, TILES, F, 2 * C, P_SIZE), P_SIZE ** -0.5, 0.375, ((0, 16), (1, 32)))
    slip_map = jnp.clip(jnp.exp(math.log(2.0) - 2.306499 * jax.random.uniform(arg_keys[1], (TILES, VMAX, P_SIZE), jnp.float32) ** block_levels(arg_keys[1], (TILES, VMAX, P_SIZE), ((0, 32), (2, 16)), -0.2, 0.2)), 0.19921875, 2.0).astype(jnp.bfloat16)
    rupture_time = jnp.clip(48.0 * jax.random.uniform(arg_keys[2], (TILES, VMAX, P_SIZE), jnp.float32) ** block_levels(arg_keys[2], (TILES, VMAX, P_SIZE), ((0, 32), (2, 16)), -0.2, 0.2), 0.0, 48.0)
    variation_ids = jax.vmap(lambda own: jax.random.permutation(own, VMAX))(jax.random.split(arg_keys[3], TILES)).reshape((TILES, VMAX)).astype(jnp.int32)
    variation_count = draw_variation_count(jax.random.fold_in(arg_keys[7], 71), 0)
    tile_rupture = place_ends(jax.random.randint(arg_keys[5], (TILES,), 0, RUPT), jax.random.fold_in(arg_keys[5], 1), 0, RUPT - 1).astype(jnp.int32)
    owner_slot = jax.random.permutation(arg_keys[6], RUPT).astype(jnp.int32)
    return {"green_tensor": green_tensor, "slip_map": slip_map, "rupture_time": rupture_time, "variation_ids": variation_ids, "variation_count": variation_count, "tile_rupture": tile_rupture, "owner_slot": owner_slot}


def inverse_table(freq_count):
    sample_count = 2 * freq_count
    wave = jnp.arange(freq_count, dtype=jnp.int32)[:, None]
    sample = jnp.arange(sample_count, dtype=jnp.int32)[None, :]
    angles = 2.0 * math.pi / sample_count * (wave * sample % sample_count).astype(jnp.float32)
    return jnp.concatenate([jnp.cos(angles), -jnp.sin(angles)], axis=0) / math.sqrt(freq_count)

def reference(green_tensor, slip_map, rupture_time, variation_ids, variation_count, tile_rupture, owner_slot):
    frequency = jnp.arange(F, dtype=jnp.float32)
    tile_total = slip_map.shape[0]
    initial = jnp.zeros((RUPT, VMAX, SITES, C, 2 * F), jnp.float32)

    def one_tile(tile_index, accumulated):
        green_tile = lax.dynamic_index_in_dim(green_tensor, tile_index, 1, keepdims=False).astype(jnp.float32)
        amplitude = slip_map[tile_index].astype(jnp.float32)
        arrival = rupture_time[tile_index]
        phases = 2.0 * math.pi / NT * frequency[:, None, None] * arrival[None]
        a_real = lax.optimization_barrier((amplitude[None] * jnp.cos(phases)).astype(jnp.bfloat16)).astype(jnp.float32)
        a_imag = lax.optimization_barrier((-amplitude[None] * jnp.sin(phases)).astype(jnp.bfloat16)).astype(jnp.float32)
        part_real = jnp.einsum('fvp,sfkp->vskf', a_real, green_tile, precision=lax.Precision.HIGHEST)
        part_imag = jnp.einsum('fvp,sfkp->vskf', a_imag, green_tile, precision=lax.Precision.HIGHEST)
        real_part = part_real[:, :, :C] - part_imag[:, :, C:]
        imag_part = part_real[:, :, C:] + part_imag[:, :, :C]
        spectrum = jnp.concatenate([real_part, imag_part], axis=-1)
        is_live = (jnp.arange(VMAX, dtype=jnp.int32) < variation_count[tile_index]).astype(jnp.float32)
        spectrum = spectrum * is_live[:, None, None, None]
        return accumulated.at[tile_rupture[tile_index], variation_ids[tile_index]].add(spectrum)
    accumulated = lax.fori_loop(0, tile_total, one_tile, initial)
    table = inverse_table(F)
    seismic = jnp.dot(accumulated.reshape(-1, 2 * F), table, precision=lax.Precision.HIGHEST, preferred_element_type=jnp.float32)
    seismic = seismic.reshape(RUPT, VMAX, SITES, C, NT)
    return jnp.zeros_like(seismic).at[owner_slot].set(seismic)
```

```python
import math

import jax
import jax.numpy as jnp
from jax import lax
from jax.experimental import pallas as pl
from jax.experimental.pallas import tpu as pltpu
from jax.sharding import PartitionSpec as P

STEP = 16


def sin_cos(angle):
    square = angle * angle
    sine = jnp.full_like(square, 1.0 / math.factorial(13))
    for order in (11, 9, 7, 5, 3, 1):
        sign = -1.0 if (order // 2) % 2 else 1.0
        sine = sine * square + sign / math.factorial(order)
    cosine = jnp.full_like(square, -1.0 / math.factorial(14))
    for order in (12, 10, 8, 6, 4, 2, 0):
        sign = -1.0 if (order // 2) % 2 else 1.0
        cosine = cosine * square + sign / math.factorial(order)
    return sine * angle, cosine


def turn(left, right):
    return (
        left[0] * right[0] - left[1] * right[1],
        left[0] * right[1] + left[1] * right[0],
    )


def pack_kernel(slip_hbm, time_hbm, out_ref, slip_ref, time_ref, sems):
    copies = [
        pltpu.make_async_copy(slip_hbm, slip_ref, sems.at[0]),
        pltpu.make_async_copy(time_hbm, time_ref, sems.at[1]),
    ]
    for copy in copies:
        copy.start()
    for copy in copies:
        copy.wait()
    slip = slip_ref[...].astype(jnp.float32).T
    arrival = time_ref[...].T
    block = jnp.concatenate([slip, arrival], axis=0)
    for peer in range(out_ref.shape[0]):
        out_ref[peer] = block


def main_kernel(maps_ref, key_ref, green_hbm, out_ref, green_ref, slip_ref, time_ref, spec_ref, sems):
    tiles, parts, freqs, points = green_ref.shape
    rows = slip_ref.shape[0] // tiles
    copies = [
        pltpu.make_async_copy(green_hbm.at[t], green_ref.at[t], sems.at[t]) for t in range(tiles)
    ]
    for copy in copies:
        copy.start()
    share = maps_ref.shape[1] // 2
    slip_ref[...] = maps_ref[:, :share, :].reshape(points, tiles * rows).T
    time_ref[...] = maps_ref[:, share:, :].reshape(points, tiles * rows).T
    chunks = freqs // STEP
    lanes = parts * STEP
    lane = lax.broadcasted_iota(jnp.int32, (2 * rows, lanes), 1) % STEP
    for t in range(tiles):
        angle = time_ref[t * rows : (t + 1) * rows, :] * (2.0 * math.pi / (2 * freqs))
        sine, cosine = sin_cos(angle)
        unit = (cosine, -sine)
        small = [None, unit]
        for b in range(2, STEP + 1):
            half = b // 2
            small.append(turn(small[half], small[b - half]))
        amplitude = slip_ref[t * rows : (t + 1) * rows, :]
        large = (amplitude, jnp.zeros_like(amplitude))
        copies[t].wait()
        for a in range(chunks):
            pieces = []
            for b in range(STEP):
                value = large if b == 0 else turn(large, small[b])
                pieces += [value[0], value[1]]
            phasor = jnp.concatenate(pieces, axis=0).astype(jnp.bfloat16)
            block = green_ref[t, :, a * STEP : (a + 1) * STEP, :].reshape(lanes, points)
            pairs = lax.dot_general(
                phasor, block, (((1,), (1,)), ((), ())), preferred_element_type=jnp.float32
            )
            own = pairs[: 2 * rows]
            for b in range(1, STEP):
                own = jnp.where(lane == b, pairs[b * 2 * rows : (b + 1) * 2 * rows], own)
            upper, lower = own[:rows], own[rows:]
            swapped = jnp.concatenate([-lower[:, lanes // 2 :], lower[:, : lanes // 2]], axis=1)
            spec_ref[t * rows : (t + 1) * rows, a * lanes : (a + 1) * lanes] = upper + swapped
            if a + 1 < chunks:
                large = turn(large, small[STEP])
    slots = out_ref.shape[0]
    chosen = lax.broadcasted_iota(jnp.int32, (slots, tiles * rows), 0) == key_ref[...]
    chosen = jnp.where(chosen, 1.0, 0.0).astype(jnp.bfloat16)
    spectrum = spec_ref[...]
    high = spectrum.astype(jnp.bfloat16)
    rest = spectrum - high.astype(jnp.float32)
    middle = rest.astype(jnp.bfloat16)
    low = (rest - middle.astype(jnp.float32)).astype(jnp.bfloat16)
    out_ref[...] = (
        jnp.dot(chosen, high, preferred_element_type=jnp.float32)
        + jnp.dot(chosen, middle, preferred_element_type=jnp.float32)
        + jnp.dot(chosen, low, preferred_element_type=jnp.float32)
    )


def final_kernel(received_ref, table_ref, out_ref):
    rows = received_ref.shape[1]
    width = received_ref.shape[2]
    total = jnp.sum(received_ref[...], axis=0)
    lanes = 6 * STEP
    chunks = width // lanes
    blocks = []
    for c in range(3):
        pieces = []
        for part in range(2):
            for a in range(chunks):
                first = a * lanes + (part * 3 + c) * STEP
                pieces.append(total[:, first : first + STEP])
        blocks.append(jnp.concatenate(pieces, axis=1))
    spectrum = jnp.concatenate(blocks, axis=0)
    out_ref[...] = jnp.dot(
        spectrum,
        table_ref[...],
        precision=lax.Precision.HIGHEST,
        preferred_element_type=jnp.float32,
    )


def inverse_table(freq_count):
    sample_count = 2 * freq_count
    wave = jnp.arange(freq_count, dtype=jnp.int32)[:, None]
    sample = jnp.arange(sample_count, dtype=jnp.int32)[None, :]
    angles = 2.0 * math.pi / sample_count * (wave * sample % sample_count).astype(jnp.float32)
    return jnp.concatenate([jnp.cos(angles), -jnp.sin(angles)], axis=0) / math.sqrt(freq_count)


def vmem():
    return pl.BlockSpec(memory_space=pltpu.VMEM)


def hbm():
    return pl.BlockSpec(memory_space=pltpu.HBM)


def in_hbm(array):
    return pltpu.with_memory_space_constraint(array, pltpu.HBM)


def per_device(
    green_tensor, slip_map, rupture_time, variation_ids, variation_count, tile_rupture, owner_slot
):
    _, tiles, freqs, parts, points = green_tensor.shape
    rows, share = slip_map.shape[1:]
    sites = points // share
    ruptures = owner_slot.shape[0]
    packed = pl.pallas_call(
        pack_kernel,
        in_specs=[hbm(), hbm()],
        out_specs=vmem(),
        out_shape=jax.ShapeDtypeStruct((sites, 2 * share, tiles * rows), jnp.float32),
        scratch_shapes=[
            pltpu.VMEM((tiles * rows, share), slip_map.dtype),
            pltpu.VMEM((tiles * rows, share), rupture_time.dtype),
            pltpu.SemaphoreType.DMA((2,)),
        ],
        compiler_params=pltpu.CompilerParams(vmem_limit_bytes=4 << 20),
        name="pack",
    )(in_hbm(slip_map.reshape(tiles * rows, share)), in_hbm(rupture_time.reshape(tiles * rows, share)))
    maps = lax.all_to_all(packed, "site", 0, 0, tiled=True)
    member = tile_rupture[:, None] == jnp.arange(ruptures, dtype=jnp.int32)[None, :]
    slot = jnp.sum(jnp.where(member, owner_slot[None, :], 0), axis=1)
    live = jnp.arange(rows, dtype=jnp.int32)[None, :] < variation_count[:, None]
    key = jnp.where(live, slot[:, None] * rows + variation_ids, -1).reshape(1, tiles * rows)
    green = jnp.transpose(green_tensor[0], (0, 2, 1, 3))
    partial = pl.pallas_call(
        main_kernel,
        in_specs=[vmem(), vmem(), hbm()],
        out_specs=vmem(),
        out_shape=jax.ShapeDtypeStruct((ruptures * rows, freqs * parts), jnp.float32),
        scratch_shapes=[
            pltpu.VMEM((tiles, parts, freqs, points), jnp.bfloat16),
            pltpu.VMEM((tiles * rows, points), jnp.float32),
            pltpu.VMEM((tiles * rows, points), jnp.float32),
            pltpu.VMEM((tiles * rows, freqs * parts), jnp.float32),
            pltpu.SemaphoreType.DMA((tiles,)),
        ],
        compiler_params=pltpu.CompilerParams(vmem_limit_bytes=16 << 20),
        name="spectra",
    )(maps, key, in_hbm(green))
    received = lax.all_to_all(
        partial.reshape(ruptures, rows, freqs * parts), "fault", 0, 0, tiled=True
    )
    seismic = pl.pallas_call(
        final_kernel,
        in_specs=[vmem(), vmem()],
        out_specs=vmem(),
        out_shape=jax.ShapeDtypeStruct((3 * rows, 2 * freqs), jnp.float32),
        compiler_params=pltpu.CompilerParams(vmem_limit_bytes=6 << 20),
        name="invert",
    )(received, inverse_table(freqs))
    seismic = seismic.reshape(3, rows, 2 * freqs).transpose(1, 0, 2)
    return seismic.reshape(1, rows, 1, 3, 2 * freqs)


def solution(mesh):
    placed = (
        P("site", "fault", None, None, None),
        P("fault", None, "site"),
        P("fault", None, "site"),
        P("fault", None),
        P("fault"),
        P("fault"),
        P(),
    )
    return jax.shard_map(
        per_device,
        mesh=mesh,
        in_specs=placed,
        out_specs=P("fault", None, "site", None, None),
        check_vma=False,
    )
```

```python
import math

import jax
import jax.numpy as jnp
from jax import lax
from jax.experimental import pallas as pl
from jax.experimental.pallas import tpu as pltpu
from jax.sharding import PartitionSpec as P

STEP = 16
AHEAD = 2
GROUPS = (0, 2, 6)


def sin_cos(angle):
    square = angle * angle
    sine = jnp.full_like(square, 1.0 / math.factorial(13))
    for order in (11, 9, 7, 5, 3, 1):
        sign = -1.0 if (order // 2) % 2 else 1.0
        sine = sine * square + sign / math.factorial(order)
    cosine = jnp.full_like(square, -1.0 / math.factorial(14))
    for order in (12, 10, 8, 6, 4, 2, 0):
        sign = -1.0 if (order // 2) % 2 else 1.0
        cosine = cosine * square + sign / math.factorial(order)
    return sine * angle, cosine


def turn(left, right):
    return (
        left[0] * right[0] - left[1] * right[1],
        left[0] * right[1] + left[1] * right[0],
    )


def turn_both(left, right):
    xx, yy = left[0] * right[0], left[1] * right[1]
    xy, yx = left[0] * right[1], left[1] * right[0]
    return (xx - yy, xy + yx), (xx + yy, yx - xy)


def double(unit):
    twice = unit[1] + unit[1]
    return 1.0 - twice * unit[1], twice * unit[0]


def pack_kernel(slip_hbm, time_hbm, out_hbm, slip_ref, time_ref, block_ref, sems):
    copies = [
        pltpu.make_async_copy(slip_hbm, slip_ref, sems.at[0]),
        pltpu.make_async_copy(time_hbm, time_ref, sems.at[1]),
    ]
    for copy in copies:
        copy.start()
    share = slip_ref.shape[1]
    copies[0].wait()
    block_ref[:share] = slip_ref[...].astype(jnp.float32).T
    copies[1].wait()
    block_ref[share:] = time_ref[...].T
    sends = [
        pltpu.make_async_copy(block_ref, out_hbm.at[peer], sems.at[2 + peer])
        for peer in range(out_hbm.shape[0])
    ]
    for send in sends:
        send.start()
    for send in sends:
        send.wait()


def main_kernel(maps_ref, key_ref, green_hbm, out_hbm, green_ref, slip_ref, time_ref, spec_ref, out_ref, sems):
    tiles, parts, freqs, points = green_ref.shape
    rows = slip_ref.shape[0] // tiles
    copies = [
        pltpu.make_async_copy(green_hbm.at[t], green_ref.at[t], sems.at[t]) for t in range(tiles)
    ]
    for copy in copies:
        copy.start()
    share = maps_ref.shape[1] // 2
    slip_ref[...] = maps_ref[:, :share, :].reshape(points, tiles * rows).T
    time_ref[...] = maps_ref[:, share:, :].reshape(points, tiles * rows).T
    chunks = freqs // STEP
    middle = STEP // 2
    lanes = parts * STEP
    lane = lax.broadcasted_iota(jnp.int32, (2 * rows, lanes), 1) % STEP

    def waves(t):
        angle = time_ref[t * rows : (t + 1) * rows, :] * (2.0 * math.pi / (2 * freqs))
        sine, cosine = sin_cos(angle)
        unit = {1: (cosine, -sine)}
        unit[2] = double(unit[1])
        unit[4] = double(unit[2])
        unit[5], unit[3] = turn_both(unit[4], unit[1])
        unit[6] = double(unit[3])
        unit[7] = turn(unit[4], unit[3])
        unit[8] = double(unit[4])
        unit[16] = double(unit[8])
        amplitude = slip_ref[t * rows : (t + 1) * rows, :]
        return unit, (amplitude * unit[8][0], amplitude * unit[8][1])

    ready = {t: waves(t) for t in range(min(AHEAD, tiles))}
    for t in range(tiles):
        if t in GROUPS:
            last = min([g for g in GROUPS if g > t], default=tiles)
            for copy in copies[t:last]:
                copy.wait()
        unit, center = ready.pop(t)
        if t + AHEAD < tiles:
            ready[t + AHEAD] = waves(t + AHEAD)
        for a in range(chunks):
            values = {0: center}
            for b in range(1, middle):
                values[b], values[-b] = turn_both(center, unit[b])
            values[-middle] = turn(center, (unit[middle][0], -unit[middle][1]))
            pieces = []
            for b in range(-middle, middle):
                pieces += [values[b][0], values[b][1]]
            phasor = jnp.concatenate(pieces, axis=0).astype(jnp.bfloat16)
            block = green_ref[t, :, a * STEP : (a + 1) * STEP, :].reshape(lanes, points)
            pairs = lax.dot_general(
                phasor, block, (((1,), (1,)), ((), ())), preferred_element_type=jnp.float32
            )
            own = pairs[: 2 * rows]
            for b in range(1, STEP):
                own = jnp.where(lane == b, pairs[b * 2 * rows : (b + 1) * 2 * rows], own)
            upper, lower = own[:rows], own[rows:]
            swapped = jnp.concatenate([-lower[:, lanes // 2 :], lower[:, : lanes // 2]], axis=1)
            spec_ref[t * rows : (t + 1) * rows, a * lanes : (a + 1) * lanes] = upper + swapped
            if a + 1 < chunks:
                center = turn(center, unit[STEP])
    slots = out_ref.shape[0]
    chosen = lax.broadcasted_iota(jnp.int32, (slots, tiles * rows), 0) == key_ref[...]
    chosen = jnp.where(chosen, 1.0, 0.0).astype(jnp.bfloat16)
    chosen = jnp.concatenate([chosen, chosen], axis=1)
    spectrum = spec_ref[...]
    high = spectrum.astype(jnp.bfloat16)
    low = (spectrum - high.astype(jnp.float32)).astype(jnp.bfloat16)
    both = jnp.concatenate([high, low], axis=0)
    blocks = 4
    size = slots // blocks
    sends = []
    for block in range(blocks):
        part = slice(block * size, (block + 1) * size)
        out_ref[part] = jnp.dot(chosen[part], both, preferred_element_type=jnp.float32)
        send = pltpu.make_async_copy(out_ref.at[part], out_hbm.at[part], sems.at[tiles + block])
        send.start()
        sends.append(send)
    for send in sends:
        send.wait()


def final_kernel(received_ref, table_ref, out_ref):
    rows = received_ref.shape[1]
    width = received_ref.shape[2]
    total = jnp.sum(received_ref[...], axis=0)
    lanes = 6 * STEP
    chunks = width // lanes
    blocks = []
    for c in range(3):
        pieces = []
        for part in range(2):
            for a in range(chunks):
                first = a * lanes + (part * 3 + c) * STEP
                pieces.append(total[:, first : first + STEP])
        blocks.append(jnp.concatenate(pieces, axis=1))
    spectrum = jnp.concatenate(blocks, axis=0)
    seismic = jnp.dot(
        spectrum,
        table_ref[...],
        precision=lax.Precision.HIGHEST,
        preferred_element_type=jnp.float32,
    )
    for c in range(3):
        for v in range(rows):
            out_ref[v, c] = seismic[c * rows + v : c * rows + v + 1]


def inverse_table(freq_count):
    sample_count = 2 * freq_count
    wave = jnp.arange(freq_count, dtype=jnp.int32)[:, None]
    sample = jnp.arange(sample_count, dtype=jnp.int32)[None, :]
    angles = 2.0 * math.pi / sample_count * (wave * sample % sample_count).astype(jnp.float32)
    return jnp.concatenate([jnp.cos(angles), -jnp.sin(angles)], axis=0) / math.sqrt(freq_count)


def vmem():
    return pl.BlockSpec(memory_space=pltpu.VMEM)


def hbm():
    return pl.BlockSpec(memory_space=pltpu.HBM)


def in_hbm(array):
    return pltpu.with_memory_space_constraint(array, pltpu.HBM)


def per_device(
    green_tensor, slip_map, rupture_time, variation_ids, variation_count, tile_rupture, owner_slot
):
    _, tiles, freqs, parts, points = green_tensor.shape
    rows, share = slip_map.shape[1:]
    sites = points // share
    ruptures = owner_slot.shape[0]
    packed = pl.pallas_call(
        pack_kernel,
        in_specs=[hbm(), hbm()],
        out_specs=hbm(),
        out_shape=jax.ShapeDtypeStruct((sites, 2 * share, tiles * rows), jnp.float32),
        scratch_shapes=[
            pltpu.VMEM((tiles * rows, share), slip_map.dtype),
            pltpu.VMEM((tiles * rows, share), rupture_time.dtype),
            pltpu.VMEM((2 * share, tiles * rows), jnp.float32),
            pltpu.SemaphoreType.DMA((2 + sites,)),
        ],
        compiler_params=pltpu.CompilerParams(vmem_limit_bytes=4 << 20),
        name="pack",
    )(in_hbm(slip_map.reshape(tiles * rows, share)), in_hbm(rupture_time.reshape(tiles * rows, share)))
    maps = lax.all_to_all(packed, "site", 0, 0, tiled=True)
    member = tile_rupture[:, None] == jnp.arange(ruptures, dtype=jnp.int32)[None, :]
    slot = jnp.sum(jnp.where(member, owner_slot[None, :], 0), axis=1)
    live = jnp.arange(rows, dtype=jnp.int32)[None, :] < variation_count[:, None]
    key = jnp.where(live, slot[:, None] * rows + variation_ids, -1).reshape(1, tiles * rows)
    green = jnp.transpose(green_tensor[0], (0, 2, 1, 3))
    partial = pl.pallas_call(
        main_kernel,
        in_specs=[vmem(), vmem(), hbm()],
        out_specs=hbm(),
        out_shape=jax.ShapeDtypeStruct((ruptures * rows, freqs * parts), jnp.float32),
        scratch_shapes=[
            pltpu.VMEM((tiles, parts, freqs, points), jnp.bfloat16),
            pltpu.VMEM((tiles * rows, points), jnp.float32),
            pltpu.VMEM((tiles * rows, points), jnp.float32),
            pltpu.VMEM((tiles * rows, freqs * parts), jnp.float32),
            pltpu.VMEM((ruptures * rows, freqs * parts), jnp.float32),
            pltpu.SemaphoreType.DMA((tiles + 4,)),
        ],
        compiler_params=pltpu.CompilerParams(vmem_limit_bytes=16 << 20),
        name="spectra",
    )(maps, key, in_hbm(green))
    received = lax.all_to_all(
        partial.reshape(ruptures, rows, freqs * parts), "fault", 0, 0, tiled=True
    )
    seismic = pl.pallas_call(
        final_kernel,
        in_specs=[vmem(), vmem()],
        out_specs=vmem(),
        out_shape=jax.ShapeDtypeStruct((rows, 3, 1, 2 * freqs), jnp.float32),
        compiler_params=pltpu.CompilerParams(vmem_limit_bytes=6 << 20),
        name="invert",
    )(received, inverse_table(freqs))
    return seismic.reshape(1, rows, 3, 1, 2 * freqs).transpose(0, 1, 3, 2, 4)


def solution(mesh):
    placed = (
        P("site", "fault", None, None, None),
        P("fault", None, "site"),
        P("fault", None, "site"),
        P("fault", None),
        P("fault"),
        P("fault"),
        P(),
    )
    return jax.shard_map(
        per_device,
        mesh=mesh,
        in_specs=placed,
        out_specs=P("fault", None, "site", None, None),
        check_vma=False,
    )
```

```python
import math

import jax
import jax.numpy as jnp
from jax import lax
from jax.experimental import pallas as pl
from jax.experimental.pallas import tpu as pltpu
from jax.sharding import PartitionSpec as P

STEP = 16
AHEAD = 2
EARLY = 6


def sin_cos(angle):
    square = angle * angle
    sine = jnp.full_like(square, 1.0 / math.factorial(13))
    for order in (11, 9, 7, 5, 3, 1):
        sign = -1.0 if (order // 2) % 2 else 1.0
        sine = sine * square + sign / math.factorial(order)
    cosine = jnp.full_like(square, -1.0 / math.factorial(14))
    for order in (12, 10, 8, 6, 4, 2, 0):
        sign = -1.0 if (order // 2) % 2 else 1.0
        cosine = cosine * square + sign / math.factorial(order)
    return sine * angle, cosine


def turn(left, right):
    return (
        left[0] * right[0] - left[1] * right[1],
        left[0] * right[1] + left[1] * right[0],
    )


def turn_both(left, right):
    xx, yy = left[0] * right[0], left[1] * right[1]
    xy, yx = left[0] * right[1], left[1] * right[0]
    return (xx - yy, xy + yx), (xx + yy, yx - xy)


def double(unit):
    twice = unit[1] + unit[1]
    return 1.0 - twice * unit[1], twice * unit[0]


def pack_kernel(slip_hbm, time_hbm, out_hbm, slip_ref, time_ref, block_ref, sems):
    copies = [
        pltpu.make_async_copy(slip_hbm, slip_ref, sems.at[0]),
        pltpu.make_async_copy(time_hbm, time_ref, sems.at[1]),
    ]
    for copy in copies:
        copy.start()
    share = slip_ref.shape[1]
    copies[0].wait()
    block_ref[:share] = slip_ref[...].astype(jnp.float32).T
    copies[1].wait()
    block_ref[share:] = time_ref[...].T
    sends = [
        pltpu.make_async_copy(block_ref, out_hbm.at[peer], sems.at[2 + peer])
        for peer in range(out_hbm.shape[0])
    ]
    for send in sends:
        send.start()
    for send in sends:
        send.wait()


def load_kernel(green_hbm, green_ref, sem):
    copy = pltpu.make_async_copy(green_hbm.at[: green_ref.shape[0]], green_ref, sem)
    copy.start()
    copy.wait()


def main_kernel(maps_ref, key_ref, first_ref, green_hbm, out_ref, green_ref, slip_ref, time_ref, spec_ref, sems):
    tiles, parts, freqs, points = green_hbm.shape
    early = first_ref.shape[0]
    rows = slip_ref.shape[0] // tiles
    copies = {
        t: pltpu.make_async_copy(green_hbm.at[t], green_ref.at[t - early], sems.at[t - early])
        for t in range(early, tiles)
    }
    for copy in copies.values():
        copy.start()
    share = maps_ref.shape[1] // 2
    slip_ref[...] = maps_ref[:, :share, :].reshape(points, tiles * rows).T
    time_ref[...] = maps_ref[:, share:, :].reshape(points, tiles * rows).T
    chunks = freqs // STEP
    middle = STEP // 2
    lanes = parts * STEP
    lane = lax.broadcasted_iota(jnp.int32, (2 * rows, lanes), 1) % STEP

    def waves(t):
        angle = time_ref[t * rows : (t + 1) * rows, :] * (2.0 * math.pi / (2 * freqs))
        sine, cosine = sin_cos(angle)
        unit = {1: (cosine, -sine)}
        unit[2] = double(unit[1])
        unit[4] = double(unit[2])
        unit[5], unit[3] = turn_both(unit[4], unit[1])
        unit[6] = double(unit[3])
        unit[7] = turn(unit[4], unit[3])
        unit[8] = double(unit[4])
        unit[16] = double(unit[8])
        amplitude = slip_ref[t * rows : (t + 1) * rows, :]
        return unit, (amplitude * unit[8][0], amplitude * unit[8][1])

    def keep():
        for t, a in list(done):
            spec_ref[t * rows : (t + 1) * rows, a * lanes : (a + 1) * lanes] = done.pop((t, a))

    done = {}
    ready = {t: waves(t) for t in range(min(AHEAD, tiles))}
    for t in range(tiles):
        if t == early:
            for copy in copies.values():
                copy.wait()
        keep()
        unit, center = ready.pop(t)
        if t + AHEAD < tiles:
            ready[t + AHEAD] = waves(t + AHEAD)
        for a in range(chunks):
            values = {0: center}
            for b in range(1, middle):
                values[b], values[-b] = turn_both(center, unit[b])
            values[-middle] = turn(center, (unit[middle][0], -unit[middle][1]))
            pieces = []
            for b in range(-middle, middle):
                pieces += [values[b][0], values[b][1]]
            phasor = jnp.concatenate(pieces, axis=0).astype(jnp.bfloat16)
            source = first_ref.at[t] if t < early else green_ref.at[t - early]
            block = source[:, a * STEP : (a + 1) * STEP, :].reshape(lanes, points)
            pairs = lax.dot_general(
                phasor, block, (((1,), (1,)), ((), ())), preferred_element_type=jnp.float32
            )
            own = pairs[: 2 * rows]
            for b in range(1, STEP):
                own = jnp.where(lane == b, pairs[b * 2 * rows : (b + 1) * 2 * rows], own)
            upper, lower = own[:rows], own[rows:]
            swapped = jnp.concatenate([-lower[:, lanes // 2 :], lower[:, : lanes // 2]], axis=1)
            done[t, a] = upper + swapped
            if a + 1 < chunks:
                center = turn(center, unit[STEP])
    keep()
    slots, width = out_ref.shape
    chosen = lax.broadcasted_iota(jnp.int32, (slots, tiles * rows), 0) == key_ref[...]
    chosen = jnp.where(chosen, 1.0, 0.0).astype(jnp.bfloat16)
    chosen = jnp.concatenate([chosen, chosen], axis=1)
    for first in range(0, width, 256):
        part = slice(first, min(first + 256, width))
        spectrum = spec_ref[:, part]
        high = spectrum.astype(jnp.bfloat16)
        low = (spectrum - high.astype(jnp.float32)).astype(jnp.bfloat16)
        both = jnp.concatenate([high, low], axis=0)
        out_ref[:, part] = jnp.dot(chosen, both, preferred_element_type=jnp.float32)


def final_kernel(received_ref, table_ref, out_ref):
    rows = received_ref.shape[1]
    width = received_ref.shape[2]
    total = jnp.sum(received_ref[...], axis=0)
    lanes = 6 * STEP
    chunks = width // lanes
    blocks = []
    for c in range(3):
        pieces = []
        for part in range(2):
            for a in range(chunks):
                first = a * lanes + (part * 3 + c) * STEP
                pieces.append(total[:, first : first + STEP])
        blocks.append(jnp.concatenate(pieces, axis=1))
    spectrum = jnp.concatenate(blocks, axis=0)
    seismic = jnp.dot(
        spectrum,
        table_ref[...],
        precision=lax.Precision.HIGHEST,
        preferred_element_type=jnp.float32,
    )
    for c in range(3):
        for v in range(rows):
            out_ref[v, c] = seismic[c * rows + v : c * rows + v + 1]


def inverse_table(freq_count):
    sample_count = 2 * freq_count
    wave = jnp.arange(freq_count, dtype=jnp.int32)[:, None]
    sample = jnp.arange(sample_count, dtype=jnp.int32)[None, :]
    angles = 2.0 * math.pi / sample_count * (wave * sample % sample_count).astype(jnp.float32)
    return jnp.concatenate([jnp.cos(angles), -jnp.sin(angles)], axis=0) / math.sqrt(freq_count)


def vmem():
    return pl.BlockSpec(memory_space=pltpu.VMEM)


def hbm():
    return pl.BlockSpec(memory_space=pltpu.HBM)


def in_hbm(array):
    return pltpu.with_memory_space_constraint(array, pltpu.HBM)


def per_device(
    green_tensor, slip_map, rupture_time, variation_ids, variation_count, tile_rupture, owner_slot
):
    _, tiles, freqs, parts, points = green_tensor.shape
    rows, share = slip_map.shape[1:]
    sites = points // share
    ruptures = owner_slot.shape[0]
    packed = pl.pallas_call(
        pack_kernel,
        in_specs=[hbm(), hbm()],
        out_specs=hbm(),
        out_shape=jax.ShapeDtypeStruct((sites, 2 * share, tiles * rows), jnp.float32),
        scratch_shapes=[
            pltpu.VMEM((tiles * rows, share), slip_map.dtype),
            pltpu.VMEM((tiles * rows, share), rupture_time.dtype),
            pltpu.VMEM((2 * share, tiles * rows), jnp.float32),
            pltpu.SemaphoreType.DMA((2 + sites,)),
        ],
        compiler_params=pltpu.CompilerParams(vmem_limit_bytes=4 << 20),
        name="pack",
    )(in_hbm(slip_map.reshape(tiles * rows, share)), in_hbm(rupture_time.reshape(tiles * rows, share)))
    maps = lax.all_to_all(packed, "site", 0, 0, tiled=True)
    member = tile_rupture[:, None] == jnp.arange(ruptures, dtype=jnp.int32)[None, :]
    slot = jnp.sum(jnp.where(member, owner_slot[None, :], 0), axis=1)
    live = jnp.arange(rows, dtype=jnp.int32)[None, :] < variation_count[:, None]
    key = jnp.where(live, slot[:, None] * rows + variation_ids, -1).reshape(1, tiles * rows)
    green = in_hbm(jnp.transpose(green_tensor[0], (0, 2, 1, 3)))
    early = min(EARLY, tiles // 2)
    first = pl.pallas_call(
        load_kernel,
        in_specs=[hbm()],
        out_specs=vmem(),
        out_shape=jax.ShapeDtypeStruct((early, *green.shape[1:]), green.dtype),
        scratch_shapes=[pltpu.SemaphoreType.DMA(())],
        compiler_params=pltpu.CompilerParams(vmem_limit_bytes=4 << 20),
        name="load",
    )(green)
    partial = pl.pallas_call(
        main_kernel,
        in_specs=[vmem(), vmem(), vmem(), hbm()],
        out_specs=vmem(),
        out_shape=jax.ShapeDtypeStruct((ruptures * rows, freqs * parts), jnp.float32),
        scratch_shapes=[
            pltpu.VMEM((tiles - early, parts, freqs, points), jnp.bfloat16),
            pltpu.VMEM((tiles * rows, points), jnp.float32),
            pltpu.VMEM((tiles * rows, points), jnp.float32),
            pltpu.VMEM((tiles * rows, freqs * parts), jnp.float32),
            pltpu.SemaphoreType.DMA((tiles - early,)),
        ],
        compiler_params=pltpu.CompilerParams(vmem_limit_bytes=16 << 20),
        name="spectra",
    )(maps, key, first, green)
    partial, table = lax.optimization_barrier((partial, inverse_table(freqs)))
    received = lax.all_to_all(
        partial.reshape(ruptures, rows, freqs * parts), "fault", 0, 0, tiled=True
    )
    seismic = pl.pallas_call(
        final_kernel,
        in_specs=[vmem(), vmem()],
        out_specs=vmem(),
        out_shape=jax.ShapeDtypeStruct((rows, 3, 1, 2 * freqs), jnp.float32),
        compiler_params=pltpu.CompilerParams(vmem_limit_bytes=6 << 20),
        name="invert",
    )(received, table)
    return seismic.reshape(1, rows, 3, 1, 2 * freqs).transpose(0, 1, 3, 2, 4)


def solution(mesh):
    placed = (
        P("site", "fault", None, None, None),
        P("fault", None, "site"),
        P("fault", None, "site"),
        P("fault", None),
        P("fault"),
        P("fault"),
        P(),
    )
    return jax.shard_map(
        per_device,
        mesh=mesh,
        in_specs=placed,
        out_specs=P("fault", None, "site", None, None),
        check_vma=False,
    )
```

```python
import math

import jax
import jax.numpy as jnp
from jax import lax
from jax.experimental import pallas as pl
from jax.experimental.pallas import tpu as pltpu
from jax.sharding import PartitionSpec as P

STEP = 16
AHEAD = 2
EARLY = 6


def sin_cos(angle):
    square = angle * angle
    sine = jnp.full_like(square, 1.0 / math.factorial(13))
    for order in (11, 9, 7, 5, 3, 1):
        sign = -1.0 if (order // 2) % 2 else 1.0
        sine = sine * square + sign / math.factorial(order)
    cosine = jnp.full_like(square, -1.0 / math.factorial(14))
    for order in (12, 10, 8, 6, 4, 2, 0):
        sign = -1.0 if (order // 2) % 2 else 1.0
        cosine = cosine * square + sign / math.factorial(order)
    return sine * angle, cosine


def turn(left, right):
    return (
        left[0] * right[0] - left[1] * right[1],
        left[0] * right[1] + left[1] * right[0],
    )


def turn_both(left, right):
    xx, yy = left[0] * right[0], left[1] * right[1]
    xy, yx = left[0] * right[1], left[1] * right[0]
    return (xx - yy, xy + yx), (xx + yy, yx - xy)


def double(unit):
    twice = unit[1] + unit[1]
    return 1.0 - twice * unit[1], twice * unit[0]


def two_terms(value):
    high = value.astype(jnp.bfloat16)
    low = (value - high.astype(jnp.float32)).astype(jnp.bfloat16)
    return jnp.concatenate([high, low], axis=0)


def pack_kernel(slip_hbm, time_hbm, out_hbm, slip_ref, time_ref, block_ref, sems):
    copies = [
        pltpu.make_async_copy(slip_hbm, slip_ref, sems.at[0]),
        pltpu.make_async_copy(time_hbm, time_ref, sems.at[1]),
    ]
    for copy in copies:
        copy.start()
    share = slip_ref.shape[1]
    copies[0].wait()
    block_ref[:share] = slip_ref[...].astype(jnp.float32).T
    copies[1].wait()
    block_ref[share:] = time_ref[...].T
    sends = [
        pltpu.make_async_copy(block_ref, out_hbm.at[peer], sems.at[2 + peer])
        for peer in range(out_hbm.shape[0])
    ]
    for send in sends:
        send.start()
    for send in sends:
        send.wait()


def load_kernel(green_hbm, green_ref, sem):
    copy = pltpu.make_async_copy(green_hbm.at[: green_ref.shape[0]], green_ref, sem)
    copy.start()
    copy.wait()


def main_kernel(maps_ref, key_ref, first_ref, green_hbm, out_ref, green_ref, slip_ref, time_ref, spec_ref, sems):
    tiles, parts, freqs, points = green_hbm.shape
    early = first_ref.shape[0]
    rows = slip_ref.shape[0] // tiles
    copies = {
        t: pltpu.make_async_copy(green_hbm.at[t], green_ref.at[t - early], sems.at[t - early])
        for t in range(early, tiles)
    }
    for copy in copies.values():
        copy.start()
    share = maps_ref.shape[1] // 2
    slip_ref[...] = maps_ref[:, :share, :].reshape(points, tiles * rows).T
    time_ref[...] = maps_ref[:, share:, :].reshape(points, tiles * rows).T
    chunks = freqs // STEP
    middle = STEP // 2
    lanes = parts * STEP
    lane = lax.broadcasted_iota(jnp.int32, (2 * rows, lanes), 1) % STEP

    def waves(t):
        angle = time_ref[t * rows : (t + 1) * rows, :] * (2.0 * math.pi / (2 * freqs))
        sine, cosine = sin_cos(angle)
        unit = {1: (cosine, -sine)}
        unit[2] = double(unit[1])
        unit[4] = double(unit[2])
        unit[5], unit[3] = turn_both(unit[4], unit[1])
        unit[6] = double(unit[3])
        unit[7] = turn(unit[4], unit[3])
        unit[8] = double(unit[4])
        unit[16] = double(unit[8])
        amplitude = slip_ref[t * rows : (t + 1) * rows, :]
        return unit, (amplitude * unit[8][0], amplitude * unit[8][1])

    def keep():
        for t, a in list(done):
            spec_ref[t * rows : (t + 1) * rows, a * lanes : (a + 1) * lanes] = done.pop((t, a))

    done = {}
    ready = {t: waves(t) for t in range(min(AHEAD, tiles))}
    for t in range(tiles):
        if t == early:
            for copy in copies.values():
                copy.wait()
        keep()
        unit, center = ready.pop(t)
        if t + AHEAD < tiles:
            ready[t + AHEAD] = waves(t + AHEAD)
        for a in range(chunks):
            values = {0: center}
            for b in range(1, middle):
                values[b], values[-b] = turn_both(center, unit[b])
            values[-middle] = turn(center, (unit[middle][0], -unit[middle][1]))
            pieces = []
            for b in range(-middle, middle):
                pieces += [values[b][0], values[b][1]]
            phasor = jnp.concatenate(pieces, axis=0).astype(jnp.bfloat16)
            source = first_ref.at[t] if t < early else green_ref.at[t - early]
            block = source[:, a * STEP : (a + 1) * STEP, :].reshape(lanes, points)
            pairs = lax.dot_general(
                phasor, block, (((1,), (1,)), ((), ())), preferred_element_type=jnp.float32
            )
            own = pairs[: 2 * rows]
            for b in range(1, STEP):
                own = jnp.where(lane == b, pairs[b * 2 * rows : (b + 1) * 2 * rows], own)
            upper, lower = own[:rows], own[rows:]
            swapped = jnp.concatenate([-lower[:, lanes // 2 :], lower[:, : lanes // 2]], axis=1)
            done[t, a] = upper + swapped
            if a + 1 < chunks:
                center = turn(center, unit[STEP])
    keep()
    width = spec_ref.shape[1]
    slots = out_ref.shape[0] * 128 // (rows * width)
    height = rows * width // 128
    half = rows // 2
    row = lax.broadcasted_iota(jnp.int32, (slots * rows, tiles * rows), 0)
    turned = row // rows * rows + (row % rows + (row // rows) % 2 * half) % rows
    key = key_ref[...]
    chosen = jnp.where(turned == key, 1.0, 0.0).astype(jnp.bfloat16)
    chosen = jnp.concatenate([chosen, chosen], axis=1)
    whole = width // 128 * 128
    for first in range(0, whole, 256):
        both = two_terms(spec_ref[:, first : first + 256])
        routed = jnp.dot(chosen, both, preferred_element_type=jnp.float32)
        for slot in range(slots):
            for block in range(2):
                base = slot * height + (first // 128 + block) * rows
                piece = routed[slot * rows : (slot + 1) * rows, block * 128 : (block + 1) * 128]
                if slot % 2:
                    out_ref[base : base + half] = piece[half:]
                    out_ref[base + half : base + rows] = piece[:half]
                else:
                    out_ref[base : base + rows] = piece
    row = lax.broadcasted_iota(jnp.int32, (slots * half, tiles * rows), 0)
    lower = row // half * rows + row % half
    left = jnp.where(lower == key, 1.0, 0.0).astype(jnp.bfloat16)
    right = jnp.where(lower + half == key, 1.0, 0.0).astype(jnp.bfloat16)
    both = two_terms(spec_ref[:, whole:])
    blank = jnp.zeros_like(both)
    routed = jnp.dot(
        jnp.concatenate([left, left], axis=1),
        jnp.concatenate([both, blank], axis=1),
        preferred_element_type=jnp.float32,
    ) + jnp.dot(
        jnp.concatenate([right, right], axis=1),
        jnp.concatenate([blank, both], axis=1),
        preferred_element_type=jnp.float32,
    )
    for slot in range(slots):
        base = slot * height + height - half
        out_ref[base : base + half] = routed[slot * half : (slot + 1) * half]


def final_kernel(received_ref, table_ref, out_ref):
    rows = out_ref.shape[0]
    width = 3 * table_ref.shape[0]
    height = rows * width // 128
    pairs = received_ref[: 2 * height]
    for source in range(1, received_ref.shape[0] // (2 * height)):
        pairs += received_ref[source * 2 * height : (source + 1) * 2 * height]
    summed = pairs[:height] + pairs[height:]
    pieces = [summed[first : first + rows] for first in range(0, height - rows // 2, rows)]
    last = summed[height - rows // 2 :]
    pieces.append(jnp.concatenate([last[:, :64], last[:, 64:]], axis=0))
    total = jnp.concatenate(pieces, axis=1)
    lanes = 6 * STEP
    chunks = width // lanes
    blocks = []
    for c in range(3):
        pieces = []
        for part in range(2):
            for a in range(chunks):
                first = a * lanes + (part * 3 + c) * STEP
                pieces.append(total[:, first : first + STEP])
        blocks.append(jnp.concatenate(pieces, axis=1))
    spectrum = jnp.concatenate(blocks, axis=0)
    seismic = jnp.dot(
        spectrum,
        table_ref[...],
        precision=lax.Precision.HIGHEST,
        preferred_element_type=jnp.float32,
    )
    for c in range(3):
        for v in range(rows):
            out_ref[v, c] = seismic[c * rows + v : c * rows + v + 1]


def inverse_table(freq_count):
    sample_count = 2 * freq_count
    wave = jnp.arange(freq_count, dtype=jnp.int32)[:, None]
    sample = jnp.arange(sample_count, dtype=jnp.int32)[None, :]
    angles = 2.0 * math.pi / sample_count * (wave * sample % sample_count).astype(jnp.float32)
    return jnp.concatenate([jnp.cos(angles), -jnp.sin(angles)], axis=0) / math.sqrt(freq_count)


def vmem():
    return pl.BlockSpec(memory_space=pltpu.VMEM)


def hbm():
    return pl.BlockSpec(memory_space=pltpu.HBM)


def in_hbm(array):
    return pltpu.with_memory_space_constraint(array, pltpu.HBM)


def per_device(
    green_tensor, slip_map, rupture_time, variation_ids, variation_count, tile_rupture, owner_slot
):
    _, tiles, freqs, parts, points = green_tensor.shape
    rows, share = slip_map.shape[1:]
    sites = points // share
    ruptures = owner_slot.shape[0]
    packed = pl.pallas_call(
        pack_kernel,
        in_specs=[hbm(), hbm()],
        out_specs=hbm(),
        out_shape=jax.ShapeDtypeStruct((sites, 2 * share, tiles * rows), jnp.float32),
        scratch_shapes=[
            pltpu.VMEM((tiles * rows, share), slip_map.dtype),
            pltpu.VMEM((tiles * rows, share), rupture_time.dtype),
            pltpu.VMEM((2 * share, tiles * rows), jnp.float32),
            pltpu.SemaphoreType.DMA((2 + sites,)),
        ],
        compiler_params=pltpu.CompilerParams(vmem_limit_bytes=4 << 20),
        name="pack",
    )(in_hbm(slip_map.reshape(tiles * rows, share)), in_hbm(rupture_time.reshape(tiles * rows, share)))
    maps = lax.all_to_all(packed, "site", 0, 0, tiled=True)
    member = tile_rupture[:, None] == jnp.arange(ruptures, dtype=jnp.int32)[None, :]
    slot = jnp.sum(jnp.where(member, owner_slot[None, :], 0), axis=1)
    live = jnp.arange(rows, dtype=jnp.int32)[None, :] < variation_count[:, None]
    key = jnp.where(live, slot[:, None] * rows + variation_ids, -1).reshape(1, tiles * rows)
    green = in_hbm(jnp.transpose(green_tensor[0], (0, 2, 1, 3)))
    early = min(EARLY, tiles // 2)
    first = pl.pallas_call(
        load_kernel,
        in_specs=[hbm()],
        out_specs=vmem(),
        out_shape=jax.ShapeDtypeStruct((early, *green.shape[1:]), green.dtype),
        scratch_shapes=[pltpu.SemaphoreType.DMA(())],
        compiler_params=pltpu.CompilerParams(vmem_limit_bytes=4 << 20),
        name="load",
    )(green)
    partial = pl.pallas_call(
        main_kernel,
        in_specs=[vmem(), vmem(), vmem(), hbm()],
        out_specs=vmem(),
        out_shape=jax.ShapeDtypeStruct((ruptures * rows * freqs * parts // 128, 128), jnp.float32),
        scratch_shapes=[
            pltpu.VMEM((tiles - early, parts, freqs, points), jnp.bfloat16),
            pltpu.VMEM((tiles * rows, points), jnp.float32),
            pltpu.VMEM((tiles * rows, points), jnp.float32),
            pltpu.VMEM((tiles * rows, freqs * parts), jnp.float32),
            pltpu.SemaphoreType.DMA((tiles - early,)),
        ],
        compiler_params=pltpu.CompilerParams(vmem_limit_bytes=16 << 20),
        name="spectra",
    )(maps, key, first, green)
    partial, table = lax.optimization_barrier((partial, inverse_table(freqs)))
    received = lax.all_to_all(
        partial.reshape(ruptures, -1, rows // 2, 128), "fault", 0, 0, tiled=True
    ).reshape(-1, 128)
    seismic = pl.pallas_call(
        final_kernel,
        in_specs=[vmem(), vmem()],
        out_specs=vmem(),
        out_shape=jax.ShapeDtypeStruct((rows, 3, 1, 2 * freqs), jnp.float32),
        compiler_params=pltpu.CompilerParams(vmem_limit_bytes=6 << 20),
        name="invert",
    )(received, table)
    return seismic.reshape(1, rows, 3, 1, 2 * freqs).transpose(0, 1, 3, 2, 4)


def solution(mesh):
    placed = (
        P("site", "fault", None, None, None),
        P("fault", None, "site"),
        P("fault", None, "site"),
        P("fault", None),
        P("fault"),
        P("fault"),
        P(),
    )
    return jax.shard_map(
        per_device,
        mesh=mesh,
        in_specs=placed,
        out_specs=P("fault", None, "site", None, None),
        check_vma=False,
    )
```

```python
import math

import jax
import jax.numpy as jnp
from jax import lax
from jax.experimental import pallas as pl
from jax.experimental.pallas import tpu as pltpu
from jax.sharding import PartitionSpec as P

STEP = 16
AHEAD = 2
EARLY = 6
SENDS = 2


def sin_cos(angle):
    square = angle * angle
    sine = jnp.full_like(square, 1.0 / math.factorial(13))
    for order in (11, 9, 7, 5, 3, 1):
        sign = -1.0 if (order // 2) % 2 else 1.0
        sine = sine * square + sign / math.factorial(order)
    cosine = jnp.full_like(square, -1.0 / math.factorial(14))
    for order in (12, 10, 8, 6, 4, 2, 0):
        sign = -1.0 if (order // 2) % 2 else 1.0
        cosine = cosine * square + sign / math.factorial(order)
    return sine * angle, cosine


def turn(left, right):
    return (
        left[0] * right[0] - left[1] * right[1],
        left[0] * right[1] + left[1] * right[0],
    )


def turn_both(left, right):
    xx, yy = left[0] * right[0], left[1] * right[1]
    xy, yx = left[0] * right[1], left[1] * right[0]
    return (xx - yy, xy + yx), (xx + yy, yx - xy)


def double(unit):
    twice = unit[1] + unit[1]
    return 1.0 - twice * unit[1], twice * unit[0]


def two_terms(value):
    high = value.astype(jnp.bfloat16)
    low = (value - high.astype(jnp.float32)).astype(jnp.bfloat16)
    return jnp.concatenate([high, low], axis=0)


def pack_kernel(slip_hbm, time_hbm, out_hbm, slip_ref, time_ref, block_ref, sems):
    copies = [
        pltpu.make_async_copy(time_hbm, time_ref, sems.at[0]),
        pltpu.make_async_copy(slip_hbm, slip_ref, sems.at[1]),
    ]
    for copy in copies:
        copy.start()
    for copy in copies:
        copy.wait()
    block = jnp.concatenate([slip_ref[...].astype(jnp.float32).T, time_ref[...].T], axis=0)
    peers = out_hbm.shape[0]
    sends = []
    for first in range(0, peers, peers // SENDS):
        part = pl.ds(first, peers // SENDS)
        for peer in range(first, first + peers // SENDS):
            block_ref[peer] = block
        sends.append(
            pltpu.make_async_copy(block_ref.at[part], out_hbm.at[part], sems.at[2 + len(sends)])
        )
        sends[-1].start()
    for send in sends:
        send.wait()


def load_kernel(green_hbm, green_ref, sem):
    copy = pltpu.make_async_copy(green_hbm.at[: green_ref.shape[0]], green_ref, sem)
    copy.start()
    copy.wait()


def main_kernel(maps_ref, key_ref, first_ref, green_hbm, out_ref, green_ref, slip_ref, time_ref, spec_ref, sems):
    tiles, parts, freqs, points = green_hbm.shape
    early = first_ref.shape[0]
    rows = slip_ref.shape[0] // tiles
    copies = {
        t: pltpu.make_async_copy(green_hbm.at[t], green_ref.at[t - early], sems.at[t - early])
        for t in range(early, tiles)
    }
    for copy in copies.values():
        copy.start()
    share = maps_ref.shape[1] // 2
    slip_ref[...] = maps_ref[:, :share, :].reshape(points, tiles * rows).T
    time_ref[...] = maps_ref[:, share:, :].reshape(points, tiles * rows).T
    chunks = freqs // STEP
    middle = STEP // 2
    lanes = parts * STEP
    lane = lax.broadcasted_iota(jnp.int32, (2 * rows, lanes), 1) % STEP

    def waves(t):
        angle = time_ref[t * rows : (t + 1) * rows, :] * (2.0 * math.pi / (2 * freqs))
        sine, cosine = sin_cos(angle)
        unit = {1: (cosine, -sine)}
        unit[2] = double(unit[1])
        unit[4] = double(unit[2])
        unit[5], unit[3] = turn_both(unit[4], unit[1])
        unit[6] = double(unit[3])
        unit[7] = turn(unit[4], unit[3])
        unit[8] = double(unit[4])
        unit[16] = double(unit[8])
        amplitude = slip_ref[t * rows : (t + 1) * rows, :]
        return unit, (amplitude * unit[8][0], amplitude * unit[8][1])

    def keep():
        for t, a in list(done):
            spec_ref[t * rows : (t + 1) * rows, a * lanes : (a + 1) * lanes] = done.pop((t, a))

    done = {}
    ready = {t: waves(t) for t in range(min(AHEAD, tiles))}
    for t in range(tiles):
        if t == early:
            for copy in copies.values():
                copy.wait()
        keep()
        unit, center = ready.pop(t)
        if t + AHEAD < tiles:
            ready[t + AHEAD] = waves(t + AHEAD)
        for a in range(chunks):
            values = {0: center}
            for b in range(1, middle):
                values[b], values[-b] = turn_both(center, unit[b])
            values[-middle] = turn(center, (unit[middle][0], -unit[middle][1]))
            pieces = []
            for b in range(-middle, middle):
                pieces += [values[b][0], values[b][1]]
            phasor = jnp.concatenate(pieces, axis=0).astype(jnp.bfloat16)
            source = first_ref.at[t] if t < early else green_ref.at[t - early]
            block = source[:, a * STEP : (a + 1) * STEP, :].reshape(lanes, points)
            pairs = lax.dot_general(
                phasor, block, (((1,), (1,)), ((), ())), preferred_element_type=jnp.float32
            )
            own = pairs[: 2 * rows]
            for b in range(1, STEP):
                own = jnp.where(lane == b, pairs[b * 2 * rows : (b + 1) * 2 * rows], own)
            upper, lower = own[:rows], own[rows:]
            swapped = jnp.concatenate([-lower[:, lanes // 2 :], lower[:, : lanes // 2]], axis=1)
            done[t, a] = upper + swapped
            if a + 1 < chunks:
                center = turn(center, unit[STEP])
    keep()
    width = spec_ref.shape[1]
    slots = out_ref.shape[0] * 128 // (rows * width)
    height = rows * width // 128
    half = rows // 2
    row = lax.broadcasted_iota(jnp.int32, (slots * rows, tiles * rows), 0)
    turned = row // rows * rows + (row % rows + (row // rows) % 2 * half) % rows
    key = key_ref[...]
    chosen = jnp.where(turned == key, 1.0, 0.0).astype(jnp.bfloat16)
    chosen = jnp.concatenate([chosen, chosen], axis=1)
    whole = width // 128 * 128
    for first in range(0, whole, 256):
        both = two_terms(spec_ref[:, first : first + 256])
        routed = jnp.dot(chosen, both, preferred_element_type=jnp.float32)
        for slot in range(slots):
            for block in range(2):
                base = slot * height + (first // 128 + block) * rows
                piece = routed[slot * rows : (slot + 1) * rows, block * 128 : (block + 1) * 128]
                if slot % 2:
                    out_ref[base : base + half] = piece[half:]
                    out_ref[base + half : base + rows] = piece[:half]
                else:
                    out_ref[base : base + rows] = piece
    row = lax.broadcasted_iota(jnp.int32, (slots * half, tiles * rows), 0)
    lower = row // half * rows + row % half
    left = jnp.where(lower == key, 1.0, 0.0).astype(jnp.bfloat16)
    right = jnp.where(lower + half == key, 1.0, 0.0).astype(jnp.bfloat16)
    both = two_terms(spec_ref[:, whole:])
    blank = jnp.zeros_like(both)
    routed = jnp.dot(
        jnp.concatenate([left, left], axis=1),
        jnp.concatenate([both, blank], axis=1),
        preferred_element_type=jnp.float32,
    ) + jnp.dot(
        jnp.concatenate([right, right], axis=1),
        jnp.concatenate([blank, both], axis=1),
        preferred_element_type=jnp.float32,
    )
    for slot in range(slots):
        base = slot * height + height - half
        out_ref[base : base + half] = routed[slot * half : (slot + 1) * half]


def final_kernel(received_ref, table_ref, out_ref):
    rows = out_ref.shape[0]
    width = 3 * table_ref.shape[0]
    height = rows * width // 128
    pairs = received_ref[: 2 * height]
    for source in range(1, received_ref.shape[0] // (2 * height)):
        pairs += received_ref[source * 2 * height : (source + 1) * 2 * height]
    summed = pairs[:height] + pairs[height:]
    pieces = [summed[first : first + rows] for first in range(0, height - rows // 2, rows)]
    last = summed[height - rows // 2 :]
    pieces.append(jnp.concatenate([last[:, :64], last[:, 64:]], axis=0))
    total = jnp.concatenate(pieces, axis=1)
    lanes = 6 * STEP
    chunks = width // lanes
    blocks = []
    for c in range(3):
        pieces = []
        for part in range(2):
            for a in range(chunks):
                first = a * lanes + (part * 3 + c) * STEP
                pieces.append(total[:, first : first + STEP])
        blocks.append(jnp.concatenate(pieces, axis=1))
    spectrum = jnp.concatenate(blocks, axis=0)
    seismic = jnp.dot(
        spectrum,
        table_ref[...],
        precision=lax.Precision.HIGHEST,
        preferred_element_type=jnp.float32,
    )
    for c in range(3):
        for v in range(rows):
            out_ref[v, c] = seismic[c * rows + v : c * rows + v + 1]


def inverse_table(freq_count):
    sample_count = 2 * freq_count
    wave = jnp.arange(freq_count, dtype=jnp.int32)[:, None]
    sample = jnp.arange(sample_count, dtype=jnp.int32)[None, :]
    angles = 2.0 * math.pi / sample_count * (wave * sample % sample_count).astype(jnp.float32)
    return jnp.concatenate([jnp.cos(angles), -jnp.sin(angles)], axis=0) / math.sqrt(freq_count)


def vmem():
    return pl.BlockSpec(memory_space=pltpu.VMEM)


def hbm():
    return pl.BlockSpec(memory_space=pltpu.HBM)


def in_hbm(array):
    return pltpu.with_memory_space_constraint(array, pltpu.HBM)


def per_device(
    green_tensor, slip_map, rupture_time, variation_ids, variation_count, tile_rupture, owner_slot
):
    _, tiles, freqs, parts, points = green_tensor.shape
    rows, share = slip_map.shape[1:]
    sites = points // share
    ruptures = owner_slot.shape[0]
    packed = pl.pallas_call(
        pack_kernel,
        in_specs=[hbm(), hbm()],
        out_specs=hbm(),
        out_shape=jax.ShapeDtypeStruct((sites, 2 * share, tiles * rows), jnp.float32),
        scratch_shapes=[
            pltpu.VMEM((tiles * rows, share), slip_map.dtype),
            pltpu.VMEM((tiles * rows, share), rupture_time.dtype),
            pltpu.VMEM((sites, 2 * share, tiles * rows), jnp.float32),
            pltpu.SemaphoreType.DMA((2 + SENDS,)),
        ],
        compiler_params=pltpu.CompilerParams(vmem_limit_bytes=4 << 20),
        name="pack",
    )(in_hbm(slip_map.reshape(tiles * rows, share)), in_hbm(rupture_time.reshape(tiles * rows, share)))
    maps = lax.all_to_all(packed, "site", 0, 0, tiled=True)
    member = tile_rupture[:, None] == jnp.arange(ruptures, dtype=jnp.int32)[None, :]
    slot = jnp.sum(jnp.where(member, owner_slot[None, :], 0), axis=1)
    live = jnp.arange(rows, dtype=jnp.int32)[None, :] < variation_count[:, None]
    key = jnp.where(live, slot[:, None] * rows + variation_ids, -1).reshape(1, tiles * rows)
    green = in_hbm(jnp.transpose(green_tensor[0], (0, 2, 1, 3)))
    early = min(EARLY, tiles // 2)
    first = pl.pallas_call(
        load_kernel,
        in_specs=[hbm()],
        out_specs=vmem(),
        out_shape=jax.ShapeDtypeStruct((early, *green.shape[1:]), green.dtype),
        scratch_shapes=[pltpu.SemaphoreType.DMA(())],
        compiler_params=pltpu.CompilerParams(vmem_limit_bytes=4 << 20),
        name="load",
    )(green)
    partial = pl.pallas_call(
        main_kernel,
        in_specs=[vmem(), vmem(), vmem(), hbm()],
        out_specs=vmem(),
        out_shape=jax.ShapeDtypeStruct((ruptures * rows * freqs * parts // 128, 128), jnp.float32),
        scratch_shapes=[
            pltpu.VMEM((tiles - early, parts, freqs, points), jnp.bfloat16),
            pltpu.VMEM((tiles * rows, points), jnp.float32),
            pltpu.VMEM((tiles * rows, points), jnp.float32),
            pltpu.VMEM((tiles * rows, freqs * parts), jnp.float32),
            pltpu.SemaphoreType.DMA((tiles - early,)),
        ],
        compiler_params=pltpu.CompilerParams(vmem_limit_bytes=16 << 20),
        name="spectra",
    )(maps, key, first, green)
    partial, table = lax.optimization_barrier((partial, inverse_table(freqs)))
    received = lax.all_to_all(
        partial.reshape(ruptures, -1, rows // 2, 128), "fault", 0, 0, tiled=True
    ).reshape(-1, 128)
    seismic = pl.pallas_call(
        final_kernel,
        in_specs=[vmem(), vmem()],
        out_specs=vmem(),
        out_shape=jax.ShapeDtypeStruct((rows, 3, 1, 2 * freqs), jnp.float32),
        compiler_params=pltpu.CompilerParams(vmem_limit_bytes=6 << 20),
        name="invert",
    )(received, table)
    return seismic.reshape(1, rows, 3, 1, 2 * freqs).transpose(0, 1, 3, 2, 4)


def solution(mesh):
    placed = (
        P("site", "fault", None, None, None),
        P("fault", None, "site"),
        P("fault", None, "site"),
        P("fault", None),
        P("fault"),
        P("fault"),
        P(),
    )
    return jax.shard_map(
        per_device,
        mesh=mesh,
        in_specs=placed,
        out_specs=P("fault", None, "site", None, None),
        check_vma=False,
    )
```
